32 devices in a mesh: row: 8 (over z, y), col: 4 (over x, core).
Axes of the slice: x: 2, y: 2, z: 4, core: 2. Of those that a mesh axis runs over, the one named last changes fastest.
Arguments:
- matrix: bfloat16 [6, 4096, 12, 2048], P(None, 'row', None, 'col'), may hold values from -6 to 6
- multiplier: bfloat16 [2, 512, 512], replicated
- checksum_weight: float32 [6, 4096], P(None, 'row')
Outputs:
- factored: bfloat16 [6, 4096, 12, 2048], P(None, 'row', None, 'col')
- group_checksum: float32 [8, 12, 2048], P('row', None, 'col')
- total_checksum: float32 [12, 2048], P(None, 'col')
The draws below stay inside these ranges and needn't reach their ends.
All inputs are finite; a program needn't handle non-finite values.
Results may differ from the reference program's by a relative error of at most 0.0056.
Values may be sent and summed in bfloat16 or wider, within the bound.
A program may use at most 256 MiB of HBM per device.

```python
import math
import jax
import jax.numpy as jnp
from jax import lax

PANEL_WIDTH = 512
ORDER = 24576
ELIMINATION_STEPS = 2
RBD = 6
CBD = 12
N_ROW = 8
N_COL = 4


def draw_multiplier(key, part):
    first_key, second_key = jax.random.split(jax.random.fold_in(key, 11))
    base = 2.0 * math.sqrt(PANEL_WIDTH)
    diagonal = jnp.exp(jax.random.uniform(first_key, (ELIMINATION_STEPS, PANEL_WIDTH), jnp.float32, math.log(0.5), math.log(2.0))) / base
    offdiag = jax.random.normal(second_key, (ELIMINATION_STEPS, PANEL_WIDTH, PANEL_WIDTH), jnp.float32) * (0.3 / (base * math.sqrt(PANEL_WIDTH)))
    identity = jnp.eye(PANEL_WIDTH, dtype=jnp.float32)
    return (offdiag + identity[None, :, :] * diagonal[:, :, None]).astype(jnp.bfloat16)


def draw_checksum_weight(key, part):
    sub_key = jax.random.fold_in(key, 23)
    group = (jnp.arange(N_ROW * PANEL_WIDTH, dtype=jnp.int32) // PANEL_WIDTH).astype(jnp.float32)
    rising = 1.0 + 2.0 * group / max(N_ROW - 1, 1)
    scale = 0.5 / math.sqrt(RBD * PANEL_WIDTH)
    values = jax.random.normal(sub_key, (RBD, N_ROW * PANEL_WIDTH), jnp.float32)
    return (values * rising[None, :] * scale).astype(jnp.float32)


def level_of(key, shape, shards, least, high):
    factor_of, own = 1.0, jax.random.fold_in(key, 6)
    for dim, parts in shards:
        draws = jnp.exp(jax.random.uniform(jax.random.fold_in(own, dim), (parts,), jnp.float32, least / len(shards), high / len(shards)))
        factor_of = factor_of * jnp.repeat(draws, shape[dim] // parts).reshape([-1 if axis == dim else 1 for axis in range(len(shape))])
    return factor_of


def gaussian(key, shape, spread, reach, shards=(), kind=jnp.bfloat16):
    values = jax.random.normal(key, shape, jnp.float32) * spread
    if len(shards) > 0:
        values = level_of(key, shape, shards, -0.22, 0.18) * values
    return jnp.clip(values, min=-reach, max=reach).astype(kind)


def setup_inputs(seed: int = 0) -> dict:
    splits = jax.random.split(jax.random.key(seed), 4)
    return {
        "matrix": gaussian(splits[0], (RBD, N_ROW * PANEL_WIDTH, CBD, N_COL * PANEL_WIDTH), 1.0, 6.0, ((1, 8), (3, 4))),
        "multiplier": draw_multiplier(jax.random.fold_in(splits[3], 71), 0),
        "checksum_weight": draw_checksum_weight(jax.random.fold_in(splits[3], 71), 0),
    }


slab_rows = 4096


def reference(matrix, multiplier, checksum_weight):
    highest_precision = lax.Precision.HIGHEST
    full_matrix_input = matrix.reshape(ORDER, ORDER)
    weight_rows = checksum_weight.reshape(ORDER)
    group_of_row = (jnp.arange(ORDER, dtype=jnp.int32) // PANEL_WIDTH) % N_ROW
    selector = (group_of_row[None, :] == jnp.arange(N_ROW, dtype=jnp.int32)[:, None]).astype(jnp.float32) * weight_rows[None, :]
    checks = jnp.dot(selector, full_matrix_input.astype(jnp.float32), precision=highest_precision, preferred_element_type=jnp.float32)
    column_ids = jnp.arange(ORDER, dtype=jnp.int32)
    for eliminate_block in range(ELIMINATION_STEPS):
        column_begin = eliminate_block * PANEL_WIDTH
        column_end = column_begin + PANEL_WIDTH
        lower_triangle = jnp.dot(full_matrix_input[column_end:, column_begin:column_end].astype(jnp.float32), multiplier[eliminate_block].astype(jnp.float32), precision=highest_precision, preferred_element_type=jnp.float32).astype(jnp.bfloat16)
        pivot_row_band = jnp.where(column_ids[None, :] >= column_end, full_matrix_input[column_begin:column_end, :].astype(jnp.float32), jnp.float32(0.0))
        summed = jnp.dot(selector[:, column_end:], lower_triangle.astype(jnp.float32), precision=highest_precision, preferred_element_type=jnp.float32)
        checks = checks - jnp.dot(summed, pivot_row_band, precision=highest_precision, preferred_element_type=jnp.float32)
        lower_f = lower_triangle.astype(jnp.float32)
        pieces = [full_matrix_input[:column_end]]
        for slab_start in range(column_end, ORDER, slab_rows):
            slab_stop = min(slab_start + slab_rows, ORDER)
            product = jnp.dot(lower_f[slab_start - column_end:slab_stop - column_end], pivot_row_band, precision=highest_precision, preferred_element_type=jnp.float32)
            pieces.append((full_matrix_input[slab_start:slab_stop].astype(jnp.float32) - product).astype(jnp.bfloat16))
        full_matrix_input = jnp.concatenate(pieces, axis=0)
        full_matrix_input = full_matrix_input.at[column_end:, column_begin:column_end].set(lower_triangle)
    factored = full_matrix_input.reshape(RBD, N_ROW * PANEL_WIDTH, CBD, N_COL * PANEL_WIDTH)
    return factored, checks.reshape(N_ROW, CBD, N_COL * PANEL_WIDTH), jnp.sum(checks, axis=0).reshape(CBD, N_COL * PANEL_WIDTH)
```

```python
import functools

import jax
import jax.numpy as jnp
from jax import lax
from jax.experimental import pallas as pl
from jax.experimental.pallas import tpu as pltpu
from jax.sharding import PartitionSpec as P

SUBS = 4
APART = 3
AHEAD = 3
MESH = pl.DeviceIdType.MESH


def parts(row_blocks, col_blocks):
    group = row_blocks // 2 if row_blocks % 2 == 0 else row_blocks
    return group, row_blocks // group, col_blocks - max(1, col_blocks // 6)


def split_rows(rows, f32, bf16):
    n = rows[0].shape[1]
    index = lax.broadcasted_iota(jnp.int32, (16, n), 0)
    out = jnp.zeros((16, n), f32)
    for i, row in enumerate(rows):
        rest = row
        for j in range(3):
            piece = rest.astype(bf16).astype(f32)
            out = jnp.where(index == 3 * i + j, jnp.broadcast_to(piece, (16, n)), out)
            rest = rest - piece
    return out.astype(bf16)


def sums_of(weights, upper, lower):
    f32 = jnp.float32
    p = jnp.dot(weights[0], upper, preferred_element_type=f32)
    p = p + jnp.dot(weights[1], lower, preferred_element_type=f32)
    return p[0:1] + p[1:2] + p[2:3], p[3:4] + p[4:5] + p[5:6]


def gather(dims, mt, mult, g, done, ubuf, lcat, lzb, cx, cub, wsplit,
           ebuf, min_, gcol, wacc, cyb, ct, cdb,
           usem, uzs, uys, lsem, lxs, lks, esem, exs, eks, insem, cs, cr):
    grid_rows, grid_cols, row_blocks, col_blocks, size = dims
    f32, bf16 = jnp.float32, jnp.bfloat16
    sub, half = size // SUBS, size // 2
    group, n_group, n_done = parts(row_blocks, col_blocks)
    me_r, me_c = lax.axis_index("row"), lax.axis_index("col")
    z, y, x, k = me_r // 2, me_r % 2, me_c // 2, me_c % 2
    depth_z, depth_x = grid_rows // 2, grid_cols // 2
    up, down, across = me_r + 2, me_r - 2, me_r + 1 - 2 * y
    beyond, before, sibling = me_c + 2, me_c - 2, me_c + 1 - 2 * k
    n_sub = SUBS * col_blocks
    n_check, n_unit = n_group * col_blocks, n_group * n_done
    zero = jnp.zeros((), bf16)

    first_l = row_blocks // 2
    t_item = [SUBS * (i + 1) for i in range(row_blocks + 1)]
    t_e = t_item[first_l]
    t_l = [t_item[a] if a < first_l else t_item[a + 1] for a in range(row_blocks)]
    t_comp = [t_e + 1 + a if a < first_l else t_item[a + 1] + 1 for a in range(row_blocks)]
    t_mine = SUBS + 2
    early = min(5, n_done) if n_group == 2 else 0
    t_early = t_e + 1 + first_l
    t_late = t_comp[-1] + 1
    t_y = t_comp[-1] + 1
    t_mid = t_y + APART * (depth_z - 1) + AHEAD + 1
    t_up = max(n_sub - 1, t_mid + AHEAD)
    n_step = max(n_sub, t_up + depth_z - 1, t_late + n_unit - early)

    def remote(ref, send, recv, axis, to, dst=None):
        return pltpu.make_async_remote_copy(
            src_ref=ref, dst_ref=ref if dst is None else dst, send_sem=send, recv_sem=recv,
            device_id={axis: to}, device_id_type=MESH)

    def u_ref(band, t):
        return ubuf.at[t // SUBS, band, pl.ds(pl.multiple_of((t % SUBS) * sub, sub), sub), :]

    def u_load(t):
        rows = pl.ds(pl.multiple_of((t % SUBS) * sub, sub), sub)
        return pltpu.make_async_copy(mt.at[0, t // SUBS, rows, :], u_ref(y, t), usem.at[y, t])

    def u_up(t):
        return remote(u_ref(y, t), uzs.at[t], usem.at[y, t], "row", up)

    def u_across(t):
        return remote(u_ref(y, t), uys.at[t], usem.at[y, t], "row", across)

    def u_other(t):
        return remote(u_ref(1 - y, t), uys.at[t], usem.at[1 - y, t], "row", across)

    def mine(t):
        return (x > 0) | (k != y) | (t >= SUBS)

    def others(t):
        return (x > 0) | (k == y) | (t >= SUBS)

    def u_sent(t):
        @pl.when(mine(t))
        def _():
            @pl.when(z < depth_z - 1)
            def _():
                u_up(t).wait_send()

            u_across(t).wait_send()

    def l_ref(band, a):
        return lcat.at[a, :, pl.ds(pl.multiple_of(band * size, size), size)]

    def l_load(a):
        return pltpu.make_async_copy(mt.at[a, 0], l_ref(k, a), lsem.at[k, a])

    def l_beyond(a):
        return remote(l_ref(k, a), lxs.at[a], lsem.at[k, a], "col", beyond)

    def l_sibling(a):
        return remote(l_ref(k, a), lks.at[a], lsem.at[k, a], "col", sibling)

    def l_other(a):
        return remote(l_ref(1 - k, a), lks.at[a], lsem.at[1 - k, a], "col", sibling)

    def relay_l(a):
        l_beyond(a).wait_recv()

        @pl.when(x < depth_x - 1)
        def _():
            l_beyond(a).start()

        l_sibling(a).start()

    def e_beyond():
        return remote(ebuf.at[1 - k], exs.at[0], esem.at[1 - k], "col", beyond)

    def e_sibling():
        return remote(ebuf.at[1 - k], eks.at[0], esem.at[1 - k], "col", sibling)

    def e_other():
        return remote(ebuf.at[k], eks.at[0], esem.at[k], "col", sibling)

    def send_e():
        @pl.when(x < depth_x - 1)
        def _():
            e_beyond().start()

        e_sibling().start()

    def c_y():
        return remote(ct, cs.at[0], cr.at[0], "row", across, cyb)

    def c_down():
        return remote(ct, cs.at[1], cr.at[1], "row", down, cdb)

    def c_up():
        return remote(cub, cs.at[2], cr.at[2], "row", up)

    def unit_of(j):
        if n_group == 1:
            return j, 0 * j
        rest = j - 2 * early
        m = jnp.where(j < early, j, jnp.where(rest < 0, j - early, early + rest // 2))
        return m, jnp.where(j < early, 0, jnp.where(rest < 0, 1, rest % 2))

    def unit_in(i):
        check = i < n_check
        m, h = unit_of(i - n_check)
        m = jnp.where(check, i // n_group, m)
        h = jnp.where(check, i % n_group, h)
        return pltpu.make_async_copy(mt.at[pl.ds(h * group, group), m], min_.at[i % 2], insem.at[i % 2])

    def next_in(i):
        @pl.when(i + 2 < n_check + n_unit)
        def _():
            unit_in(i + 2).start()

    @pl.when(z == 0)
    def _():
        @pl.loop(0, n_sub)
        def _(t):
            @pl.when(mine(t))
            def _():
                u_load(t).start()

    @pl.when(x == 0)
    def _():
        for a in range(row_blocks):
            l_load(a).start()

    unit_in(0).start()
    unit_in(1).start()

    barrier = pltpu.get_barrier_semaphore()
    i32 = jnp.int32
    for axis, to, there in (("row", up, z < depth_z - 1), ("row", down, z > 0), ("row", across, None),
                            ("col", beyond, x < depth_x - 1), ("col", before, x > 0), ("col", sibling, None)):
        if there is None:
            pl.semaphore_signal(barrier, inc=1, device_id={axis: to}, device_id_type=MESH)
        else:
            @pl.when(there)
            def _():
                pl.semaphore_signal(barrier, inc=1, device_id={axis: to}, device_id_type=MESH)

    for a in range(row_blocks):
        gcol[a] = jnp.broadcast_to(g[a:a + 1, :], (128, size)).T
    cx[...] = jnp.zeros_like(cx)
    wacc[...] = jnp.zeros_like(wacc)

    pl.semaphore_wait(barrier, 2 + (z < depth_z - 1).astype(i32) + (z > 0).astype(i32)
                      + (x < depth_x - 1).astype(i32) + (x > 0).astype(i32))

    def send_u(t):
        @pl.when(mine(t))
        def _():
            u_load(t).wait()
            u_up(t).start()
            u_across(t).start()

    @pl.when(z == 0)
    def _():
        @pl.loop(0, AHEAD)
        def _(t):
            send_u(t)

    @pl.when(x == 0)
    def _():
        for a in range(row_blocks):
            l_load(a).wait()
            if a < first_l:
                @pl.when(x < depth_x - 1)
                def _():
                    l_beyond(a).start()
            l_sibling(a).start()

    def relay_u(t):
        @pl.when((z > 0) & mine(t))
        def _():
            u_up(t).wait_recv()

            @pl.when(z < depth_z - 1)
            def _():
                u_up(t).start()

            u_across(t).start()

        @pl.when(z == 0)
        def _():
            @pl.when(t + AHEAD < n_sub)
            def _():
                send_u(t + AHEAD)

            u_sent(t)

    def other_u(t):
        @pl.when(others(t))
        def _():
            u_other(t).wait_recv()

    def check(i):
        m, h, slot = i // n_group, i % n_group, i % 2
        unit_in(i).wait()
        step = size // 8
        total = jnp.zeros((8, size), f32)
        for b in range(group):
            def body(s, acc, b=b):
                rows = pl.ds(pl.multiple_of(s * step, step), step)
                weight = gcol[h * group + b, rows, :]
                weight = jnp.concatenate([weight] * (size // 128), axis=1)
                value = min_[slot, b, rows, :].astype(f32) * weight
                return acc + jnp.sum(value.reshape(step // 8, 8, size), axis=0)
            total = lax.fori_loop(0, 8, body, total)
        next_in(i)
        cx[pl.ds(m, 1), :] += jnp.sum(total, axis=0, keepdims=True)

    def multipliers(a):
        l_other(a).wait_recv()

        @pl.when(x < depth_x - 1)
        def _():
            l_beyond(a).wait_send()

        l_sibling(a).wait_send()
        block_row = a * grid_rows + me_r
        first = jnp.dot(lcat[a, :, :size], mult[0], preferred_element_type=f32).astype(bf16)
        first = jnp.where(block_row > 0, first, zero)
        lcat[a, :, :size] = first
        product = jnp.dot(first, ebuf[0], preferred_element_type=f32)
        column = (lcat[a, :, size:].astype(f32) - product).astype(bf16)
        second = jnp.dot(column, mult[1], preferred_element_type=f32).astype(bf16)
        lcat[a, :, size:] = jnp.where(block_row > 1, second, zero)
        weights = split_rows([g[pl.ds(a, 1), :]], f32, bf16)
        wacc[...] += jnp.dot(weights, lcat[a], preferred_element_type=f32)

    def update(j):
        i = n_check + j
        m, h = unit_of(j)
        slot = i % 2
        block_col = m * grid_cols + me_c

        @pl.when(h == 0)
        def _():
            @pl.when((m > 0) | (x > 0))
            def _():
                for s in range(SUBS):
                    other_u(m * SUBS + s)

            @pl.when(z > 0)
            def _():
                for s in range(SUBS):
                    u_sent(m * SUBS + s)

            first = jnp.where(block_col > 0, ubuf[m, 0], zero)
            ubuf[m, 0] = first
            product = jnp.dot(lzb[...], first, preferred_element_type=f32)
            second = (ubuf[m, 1].astype(f32) - product).astype(bf16)
            ubuf[m, 1] = jnp.where(block_col > 1, second, zero)

        unit_in(i).wait()

        @pl.loop(0, group, unroll=True)
        def _(b):
            a = h * group + b
            for c in range(2):
                cols = slice(c * half, (c + 1) * half)
                upper = ubuf[m, :, :, cols].reshape(2 * size, half)
                product = jnp.dot(lcat[a], upper, preferred_element_type=f32)
                done[m, a, :, cols] = (min_[slot, b, :, cols].astype(f32) - product).astype(bf16)

        next_in(i)

        @pl.when(m == 0)
        def _():
            for band in range(2):
                @pl.when(me_c == band)
                def _():
                    @pl.loop(0, group)
                    def _(b):
                        a = h * group + b

                        @pl.when(a * grid_rows + me_r > band)
                        def _():
                            done[0, a] = lcat[a, :, band * size:(band + 1) * size]

    n_first = -(-n_check // 2)

    @pl.loop(0, n_step)
    def _(t):
        @pl.when(t < n_sub)
        def _():
            relay_u(t)

        @pl.when(t == t_mine)
        def _():
            @pl.when(x == 0)
            def _():
                @pl.when(k == y)
                def _():
                    for s in range(SUBS):
                        u_other(s).wait_recv()

                ebuf[1 - k] = ubuf[0, 1 - k]
                send_e()

                @pl.when(x < depth_x - 1)
                def _():
                    for a in range(first_l, row_blocks):
                        l_beyond(a).start()

        @pl.when(x > 0)
        def _():
            for a in range(row_blocks):
                @pl.when(t == t_l[a])
                def _():
                    relay_l(a)

            @pl.when(t == t_e)
            def _():
                e_beyond().wait_recv()
                send_e()

        @pl.when(t < n_first)
        def _():
            check(2 * t)
            if n_check % 2 == 0:
                check(2 * t + 1)
            else:
                @pl.when(2 * t + 1 < n_check)
                def _():
                    check(2 * t + 1)

        @pl.when(t == t_e + 1)
        def _():
            e_other().wait_recv()
            lzb[...] = jnp.dot(ebuf[1], mult[0], preferred_element_type=f32).astype(bf16)

        is_comp, a_now = t == t_comp[0], 0
        for a in range(1, row_blocks):
            a_now = jnp.where(t >= t_comp[a], a, a_now)
            is_comp = is_comp | (t == t_comp[a])

        @pl.when(is_comp)
        def _():
            multipliers(a_now)

        @pl.when(t == t_y)
        def _():
            w = wacc[0:1] + wacc[1:2] + wacc[2:3]
            cx[col_blocks:col_blocks + 1, :] = w[:, :size]
            cx[col_blocks + 1:col_blocks + 2, :] = w[:, size:]

        @pl.when(t == t_y + APART * (depth_z - 1 - z))
        def _():
            ct[...] = cx[...]

            @pl.when(z < depth_z - 1)
            def _():
                c_down().wait_recv()
                ct[...] += cdb[...]

            @pl.when(z > 0)
            def _():
                c_down().start()

            @pl.when(z == 0)
            def _():
                c_y().start()

        @pl.when(t == jnp.where(z == 0, t_mid, t_up + z - 1))
        def _():
            @pl.when(z == 0)
            def _():
                c_y().wait_recv()
                cub[...] = ct[...] + cyb[...]

            @pl.when(z > 0)
            def _():
                c_up().wait_recv()

            @pl.when(z < depth_z - 1)
            def _():
                c_up().start()

            for band in range(2):
                r = col_blocks + band
                wsplit[band] = split_rows([cx[r:r + 1, :], cub[r:r + 1, :]], f32, bf16)

        unit_now = (t >= t_late) & (t < t_late + n_unit - early)
        j_now = t - t_late + early
        if early:
            is_early = (t >= t_early) & (t < t_early + early)
            unit_now = unit_now | is_early
            j_now = jnp.where(is_early, t - t_early, j_now)

        @pl.when(unit_now)
        def _():
            update(j_now)

    @pl.loop(SUBS * n_done, n_sub)
    def _(t):
        other_u(t)

    @pl.when(z > 0)
    def _():
        @pl.loop(SUBS * n_done, n_sub)
        def _(t):
            u_sent(t)

    @pl.when(x < depth_x - 1)
    def _():
        e_beyond().wait_send()

    e_sibling().wait_send()

    @pl.when(z == 0)
    def _():
        c_y().wait_send()

    @pl.when(z > 0)
    def _():
        c_down().wait_send()

    @pl.when(z < depth_z - 1)
    def _():
        c_up().wait_send()


def finish(dims, mt, done, ubuf, lcat, lzb, crow, trow, wsplit, out, gout, tout,
           ucat, buf, insem, outsem, donesem):
    row_blocks, col_blocks, size = dims
    f32, bf16 = jnp.float32, jnp.bfloat16
    half = size // 2
    group, n_group, n_done = parts(row_blocks, col_blocks)
    units = [(m, h) for m in range(n_done, col_blocks) for h in range(n_group)]

    def unit_in(i):
        m, h = units[i]
        return pltpu.make_async_copy(mt.at[pl.ds(h * group, group), m], buf.at[i], insem.at[i])

    def unit_out(i):
        m, h = units[i]
        return pltpu.make_async_copy(buf.at[i], out.at[pl.ds(h * group, group), m], outsem.at[i])

    def done_out(m):
        return pltpu.make_async_copy(done.at[m], out.at[:, m], donesem.at[m])

    for i in range(len(units)):
        unit_in(i).start()
    for m in range(n_done):
        done_out(m).start()

    def sums(m, upper, lower):
        own, everyone = sums_of((wsplit[0], wsplit[1]), upper, lower)
        gout[m] = crow[pl.ds(m, 1), :] - own
        tout[pl.ds(m, 1), :] = trow[pl.ds(m, 1), :] - everyone

    @pl.loop(0, n_done)
    def _(m):
        sums(m, ubuf[m, 0], ubuf[m, 1])

    for i, (m, h) in enumerate(units):
        if h == 0:
            ucat[:size, :] = ubuf[m, 0]
            product = jnp.dot(lzb[...], ubuf[m, 0], preferred_element_type=f32)
            ucat[size:, :] = (ubuf[m, 1].astype(f32) - product).astype(bf16)
            sums(m, ucat[:size, :], ucat[size:, :])
        unit_in(i).wait()

        @pl.loop(0, group, unroll=True)
        def _(b):
            for c in range(2):
                cols = slice(c * half, (c + 1) * half)
                product = jnp.dot(lcat[h * group + b], ucat[:, cols], preferred_element_type=f32)
                buf[i, b, :, cols] = (buf[i, b, :, cols].astype(f32) - product).astype(bf16)

        unit_out(i).start()
    for m in range(n_done):
        done_out(m).wait()
    for i in range(len(units)):
        unit_out(i).wait()


def local(matrix, multiplier, checksum_weight):
    row_blocks, size, col_blocks, _ = matrix.shape
    grid_rows, grid_cols = lax.axis_size("row"), lax.axis_size("col")
    bf16, f32 = jnp.bfloat16, jnp.float32
    group, n_group, n_done = parts(row_blocks, col_blocks)
    n_sub = SUBS * col_blocks
    n_rest = n_group * (col_blocks - n_done)
    c_rows = -(-(col_blocks + 2) // 8) * 8
    dma = pltpu.SemaphoreType.DMA
    vmem = pl.BlockSpec(memory_space=pltpu.VMEM)
    hbm = pl.BlockSpec(memory_space=pltpu.HBM)
    tiles = matrix.transpose(0, 2, 1, 3)
    sums = pltpu.VMEM((c_rows, size), f32)
    held = pl.pallas_call(
        functools.partial(gather, (grid_rows, grid_cols, row_blocks, col_blocks, size)),
        out_shape=(
            pltpu.VMEM((n_done, row_blocks, size, size), bf16),
            pltpu.VMEM((col_blocks, 2, size, size), bf16),
            pltpu.VMEM((row_blocks, size, 2 * size), bf16),
            pltpu.VMEM((size, size), bf16),
            sums,
            sums,
            pltpu.VMEM((2, 16, size), bf16),
        ),
        in_specs=[hbm, vmem, vmem],
        out_specs=(vmem,) * 7,
        scratch_shapes=[
            pltpu.VMEM((2, size, size), bf16),
            pltpu.VMEM((2, group, size, size), bf16),
            pltpu.VMEM((row_blocks, size, 128), f32),
            pltpu.VMEM((16, 2 * size), f32),
            sums, sums, sums,
            dma((2, n_sub)), dma((n_sub,)), dma((n_sub,)),
            dma((2, row_blocks)), dma((row_blocks,)), dma((row_blocks,)),
            dma((2,)), dma((1,)), dma((1,)),
            dma((2,)), dma((3,)), dma((3,)),
        ],
        compiler_params=pltpu.CompilerParams(
            collective_id=0, has_side_effects=True, vmem_limit_bytes=12 * 1024 * 1024),
    )(tiles, multiplier, checksum_weight)
    held = [pltpu.with_memory_space_constraint(v, pltpu.VMEM) for v in held]
    out, gout, total = pl.pallas_call(
        functools.partial(finish, (row_blocks, col_blocks, size)),
        out_shape=(
            jax.ShapeDtypeStruct(tiles.shape, bf16),
            jax.ShapeDtypeStruct((col_blocks, 1, size), f32),
            jax.ShapeDtypeStruct((col_blocks, size), f32),
        ),
        in_specs=[hbm] + [vmem] * 7,
        out_specs=(hbm, vmem, vmem),
        scratch_shapes=[
            pltpu.VMEM((2 * size, size), bf16),
            pltpu.VMEM((n_rest, group, size, size), bf16),
            dma((n_rest,)), dma((n_rest,)), dma((n_done,)),
        ],
        compiler_params=pltpu.CompilerParams(vmem_limit_bytes=12 * 1024 * 1024),
    )(tiles, *held)
    return (out.transpose(0, 2, 1, 3), gout.transpose(1, 0, 2), total)


def solution(mesh):
    in_specs = (P(None, "row", None, "col"), P(), P(None, "row"))
    out_specs = (P(None, "row", None, "col"), P("row", None, "col"), P(None, "col"))
    return jax.shard_map(local, mesh=mesh, in_specs=in_specs, out_specs=out_specs, check_vma=False)
```

```python
import functools

import jax
import jax.numpy as jnp
from jax import lax
from jax.experimental import pallas as pl
from jax.experimental.pallas import tpu as pltpu
from jax.sharding import PartitionSpec as P

SUBS = 4
APART = 3
AHEAD = 3
LENT = 2
MESH = pl.DeviceIdType.MESH


def parts(row_blocks, col_blocks):
    group = row_blocks // 2 if row_blocks % 2 == 0 else row_blocks
    return group, row_blocks // group, col_blocks - 1


def split_rows(rows, f32, bf16):
    n = rows[0].shape[1]
    index = lax.broadcasted_iota(jnp.int32, (16, n), 0)
    out = jnp.zeros((16, n), f32)
    for i, row in enumerate(rows):
        rest = row
        for j in range(3):
            piece = rest.astype(bf16).astype(f32)
            out = jnp.where(index == 3 * i + j, jnp.broadcast_to(piece, (16, n)), out)
            rest = rest - piece
    return out.astype(bf16)


def sums_of(weights, upper, lower):
    f32 = jnp.float32
    p = jnp.dot(weights[0], upper, preferred_element_type=f32)
    p = p + jnp.dot(weights[1], lower, preferred_element_type=f32)
    return p[0:1] + p[1:2] + p[2:3], p[3:4] + p[4:5] + p[5:6]


def gather(dims, mt, mult_in, g_in, done, ubuf, lcat, lzb, cx, cub, wsplit, min_,
           mult, g, ebuf, gcol, wacc, cyb, ct, cdb,
           gsem, usem, uzs, uys, vbs, vxs, lsem, lxs, lks, esem, exs, eks, insem, cs, cr):
    grid_rows, grid_cols, row_blocks, col_blocks, size = dims
    f32, bf16 = jnp.float32, jnp.bfloat16
    sub, half = size // SUBS, size // 2
    group, n_group, n_done = parts(row_blocks, col_blocks)
    me_r, me_c = lax.axis_index("row"), lax.axis_index("col")
    z, y, x, k = me_r // 2, me_r % 2, me_c // 2, me_c % 2
    depth_z, depth_x = grid_rows // 2, grid_cols // 2
    up, down, across = me_r + 2, me_r - 2, me_r + 1 - 2 * y
    beyond, before, sibling = me_c + 2, me_c - 2, me_c + 1 - 2 * k
    n_sub = SUBS * col_blocks
    n_check, n_unit = n_group * col_blocks, n_group * n_done
    zero = jnp.zeros((), bf16)

    first_l = row_blocks // 2
    t_item = [SUBS * (i + 1) for i in range(row_blocks + 1)]
    t_e = t_item[first_l]
    t_l = [t_item[a] if a < first_l else t_item[a + 1] for a in range(row_blocks)]
    t_comp = [t_e + 1 + a if a < first_l else t_item[a + 1] + 1 for a in range(row_blocks)]
    t_mine = SUBS + 2
    early = min(5, n_done) if n_group == 2 else 0
    t_early = t_e + 1 + first_l
    t_late = t_comp[-1] + 2
    t_y = t_comp[-1] + 1
    t_mid = t_y + APART * (depth_z - 1) + AHEAD + 1
    t_up = max(n_sub - 1, t_mid + AHEAD)
    n_step = max(n_sub, t_up + depth_z - 1, t_late + n_unit - early)

    def remote(ref, send, recv, axis, to, dst=None):
        return pltpu.make_async_remote_copy(
            src_ref=ref, dst_ref=ref if dst is None else dst, send_sem=send, recv_sem=recv,
            device_id={axis: to}, device_id_type=MESH)

    def u_ref(band, t):
        return ubuf.at[t // SUBS, band, pl.ds(pl.multiple_of((t % SUBS) * sub, sub), sub), :]

    def u_load(t):
        rows = pl.ds(pl.multiple_of((t % SUBS) * sub, sub), sub)
        return pltpu.make_async_copy(mt.at[0, t // SUBS, rows, :], u_ref(y, t), usem.at[y, t])

    def u_up(t):
        return remote(u_ref(y, t), uzs.at[t], usem.at[y, t], "row", up)

    def u_across(t):
        return remote(u_ref(y, t), uys.at[t], usem.at[y, t], "row", across)

    def u_other(t):
        return remote(u_ref(1 - y, t), uys.at[t], usem.at[1 - y, t], "row", across)

    def lent(t):
        return (x == 1) & (k == y) & (t >= n_sub - LENT)

    def carried(t):
        return (x == 0) & (k == y) & (t >= SUBS - LENT) & (t < SUBS)

    def mine(t):
        return jnp.logical_not(lent(t)) & ((x > 0) | (k != y) | (t >= SUBS - LENT))

    def lend(s):
        t = SUBS - LENT + s
        return remote(u_ref(y, n_sub - LENT + s), vbs.at[s], usem.at[y, t], "col", before, u_ref(y, t))

    def hand_on(s):
        t = n_sub - LENT + s
        return remote(u_ref(k, SUBS - LENT + s), vxs.at[s], usem.at[k, t], "col", beyond, u_ref(k, t))

    def u_sent(t):
        @pl.when(mine(t))
        def _():
            @pl.when(z < depth_z - 1)
            def _():
                u_up(t).wait_send()

            u_across(t).wait_send()

    def l_ref(band, a):
        return lcat.at[a, :, pl.ds(pl.multiple_of(band * size, size), size)]

    def l_load(a):
        return pltpu.make_async_copy(mt.at[a, 0], l_ref(k, a), lsem.at[k, a])

    def l_beyond(a):
        return remote(l_ref(k, a), lxs.at[a], lsem.at[k, a], "col", beyond)

    def l_sibling(a):
        return remote(l_ref(k, a), lks.at[a], lsem.at[k, a], "col", sibling)

    def l_other(a):
        return remote(l_ref(1 - k, a), lks.at[a], lsem.at[1 - k, a], "col", sibling)

    def relay_l(a):
        l_beyond(a).wait_recv()

        @pl.when(x < depth_x - 1)
        def _():
            l_beyond(a).start()

        l_sibling(a).start()

    def e_beyond():
        return remote(ebuf.at[1 - k], exs.at[0], esem.at[1 - k], "col", beyond)

    def e_sibling():
        return remote(ebuf.at[1 - k], eks.at[0], esem.at[1 - k], "col", sibling)

    def e_other():
        return remote(ebuf.at[k], eks.at[0], esem.at[k], "col", sibling)

    def send_e():
        @pl.when(x < depth_x - 1)
        def _():
            e_beyond().start()

        e_sibling().start()

    def c_y():
        return remote(ct, cs.at[0], cr.at[0], "row", across, cyb)

    def c_down():
        return remote(ct, cs.at[1], cr.at[1], "row", down, cdb)

    def c_up():
        return remote(cub, cs.at[2], cr.at[2], "row", up)

    def unit_of(j):
        if n_group == 1:
            return j, 0 * j
        rest = j - 2 * early
        m = jnp.where(j < early, j, jnp.where(rest < 0, j - early, early + rest // 2))
        return m, jnp.where(j < early, 0, jnp.where(rest < 0, 1, rest % 2))

    def unit_in(i):
        check = i < n_check
        m, h = unit_of(i - n_check)
        last = i - n_check - n_unit
        m = jnp.where(check, i // n_group, jnp.where(last < 0, m, n_done))
        h = jnp.where(check, i % n_group, jnp.where(last < 0, h, last))
        return pltpu.make_async_copy(mt.at[pl.ds(h * group, group), m], min_.at[i % 2], insem.at[i % 2])

    def next_in(i):
        @pl.when(i + 2 < n_check + n_unit + n_group)
        def _():
            unit_in(i + 2).start()

    barrier = pltpu.get_barrier_semaphore()
    i32 = jnp.int32
    for axis, to, there in (("row", up, z < depth_z - 1), ("row", down, z > 0), ("row", across, None),
                            ("col", beyond, x < depth_x - 1), ("col", before, x > 0), ("col", sibling, None)):
        if there is None:
            pl.semaphore_signal(barrier, inc=1, device_id={axis: to}, device_id_type=MESH)
        else:
            @pl.when(there)
            def _():
                pl.semaphore_signal(barrier, inc=1, device_id={axis: to}, device_id_type=MESH)

    @pl.when(z == 0)
    def _():
        for t in range(n_sub - LENT, n_sub):
            u_load(t).start()

        @pl.loop(0, n_sub - LENT)
        def _(t):
            @pl.when(mine(t) & jnp.logical_not(carried(t)))
            def _():
                u_load(t).start()

    @pl.when(x == 0)
    def _():
        for a in range(row_blocks):
            l_load(a).start()

    g_load = pltpu.make_async_copy(g_in, g, gsem.at[0])
    mult_load = pltpu.make_async_copy(mult_in, mult, gsem.at[1])
    g_load.start()
    mult_load.start()
    unit_in(0).start()
    unit_in(1).start()

    g_load.wait()
    for a in range(row_blocks):
        gcol[a] = jnp.broadcast_to(g[a:a + 1, :], (128, size)).T
    cx[...] = jnp.zeros_like(cx)
    wacc[...] = jnp.zeros_like(wacc)

    pl.semaphore_wait(barrier, 2 + (z < depth_z - 1).astype(i32) + (z > 0).astype(i32)
                      + (x < depth_x - 1).astype(i32) + (x > 0).astype(i32))

    def send_u(t):
        @pl.when(mine(t))
        def _():
            u_load(t).wait()
            u_up(t).start()
            u_across(t).start()

    @pl.when((z == 0) & lent(n_sub - 1))
    def _():
        for s in range(LENT):
            t = n_sub - LENT + s
            u_load(t).wait()
            lend(s).start()
            u_across(t).start()

    @pl.when(z == 0)
    def _():
        @pl.loop(0, SUBS - LENT)
        def _(t):
            send_u(t)

    @pl.when(x == 0)
    def _():
        for a in range(row_blocks):
            l_load(a).wait()
            if a < first_l:
                @pl.when(x < depth_x - 1)
                def _():
                    l_beyond(a).start()
            l_sibling(a).start()

    @pl.when(z == 0)
    def _():
        @pl.loop(SUBS - LENT, AHEAD)
        def _(t):
            send_u(t)

    def relay_u(t):
        @pl.when((z > 0) & mine(t))
        def _():
            u_up(t).wait_recv()

            @pl.when(z < depth_z - 1)
            def _():
                u_up(t).start()

            u_across(t).start()

            @pl.when(carried(t) & (depth_x > 1))
            def _():
                hand_on(t - (SUBS - LENT)).start()

        @pl.when(z == 0)
        def _():
            @pl.when(t + AHEAD < n_sub)
            def _():
                send_u(t + AHEAD)

            u_sent(t)

    def other_u(t):
        u_other(t).wait_recv()

    def check(i):
        m, h, slot = i // n_group, i % n_group, i % 2
        unit_in(i).wait()
        step = size // 8
        total = jnp.zeros((8, size), f32)
        for b in range(group):
            def body(s, acc, b=b):
                rows = pl.ds(pl.multiple_of(s * step, step), step)
                weight = gcol[h * group + b, rows, :]
                weight = jnp.concatenate([weight] * (size // 128), axis=1)
                value = min_[slot, b, rows, :].astype(f32) * weight
                return acc + jnp.sum(value.reshape(step // 8, 8, size), axis=0)
            total = lax.fori_loop(0, 8, body, total)
        next_in(i)
        cx[pl.ds(m, 1), :] += jnp.sum(total, axis=0, keepdims=True)

    def multipliers(a):
        l_other(a).wait_recv()

        @pl.when(x < depth_x - 1)
        def _():
            l_beyond(a).wait_send()

        l_sibling(a).wait_send()
        block_row = a * grid_rows + me_r
        first = jnp.dot(lcat[a, :, :size], mult[0], preferred_element_type=f32).astype(bf16)
        first = jnp.where(block_row > 0, first, zero)
        lcat[a, :, :size] = first
        product = jnp.dot(first, ebuf[0], preferred_element_type=f32)
        column = (lcat[a, :, size:].astype(f32) - product).astype(bf16)
        second = jnp.dot(column, mult[1], preferred_element_type=f32).astype(bf16)
        lcat[a, :, size:] = jnp.where(block_row > 1, second, zero)
        weights = split_rows([g[pl.ds(a, 1), :]], f32, bf16)
        wacc[...] += jnp.dot(weights, lcat[a], preferred_element_type=f32)

    def update(j):
        i = n_check + j
        m, h = unit_of(j)
        slot = i % 2
        block_col = m * grid_cols + me_c

        @pl.when(h == 0)
        def _():
            @pl.when((m > 0) | (x > 0))
            def _():
                for s in range(SUBS):
                    other_u(m * SUBS + s)

            @pl.when(z > 0)
            def _():
                for s in range(SUBS):
                    u_sent(m * SUBS + s)

            first = jnp.where(block_col > 0, ubuf[m, 0], zero)
            ubuf[m, 0] = first
            product = jnp.dot(lzb[...], first, preferred_element_type=f32)
            second = (ubuf[m, 1].astype(f32) - product).astype(bf16)
            ubuf[m, 1] = jnp.where(block_col > 1, second, zero)

        unit_in(i).wait()

        @pl.loop(0, group, unroll=True)
        def _(b):
            a = h * group + b
            for c in range(2):
                cols = slice(c * half, (c + 1) * half)
                upper = ubuf[m, :, :, cols].reshape(2 * size, half)
                product = jnp.dot(lcat[a], upper, preferred_element_type=f32)
                done[m, a, :, cols] = (min_[slot, b, :, cols].astype(f32) - product).astype(bf16)

        next_in(i)

        @pl.when(m == 0)
        def _():
            for band in range(2):
                @pl.when(me_c == band)
                def _():
                    @pl.loop(0, group)
                    def _(b):
                        a = h * group + b

                        @pl.when(a * grid_rows + me_r > band)
                        def _():
                            done[0, a] = lcat[a, :, band * size:(band + 1) * size]

    n_first = -(-n_check // 2)

    @pl.loop(0, n_step)
    def _(t):
        @pl.when(t < n_sub)
        def _():
            relay_u(t)

        @pl.when(t == t_mine)
        def _():
            @pl.when(x == 0)
            def _():
                @pl.when(k == y)
                def _():
                    for s in range(SUBS):
                        other_u(s)

                @pl.when(k != y)
                def _():
                    for s in range(LENT):
                        other_u(SUBS - LENT + s)

                        @pl.when((z > 0) & (depth_x > 1))
                        def _():
                            hand_on(s).start()

                ebuf[1 - k] = ubuf[0, 1 - k]
                send_e()

                @pl.when(x < depth_x - 1)
                def _():
                    for a in range(first_l, row_blocks):
                        l_beyond(a).start()

        @pl.when(x > 0)
        def _():
            for a in range(row_blocks):
                @pl.when(t == t_l[a])
                def _():
                    relay_l(a)

            @pl.when(t == t_e)
            def _():
                e_beyond().wait_recv()
                send_e()

        @pl.when(t < n_first)
        def _():
            check(2 * t)
            if n_check % 2 == 0:
                check(2 * t + 1)
            else:
                @pl.when(2 * t + 1 < n_check)
                def _():
                    check(2 * t + 1)

        @pl.when(t == t_e + 1)
        def _():
            e_other().wait_recv()
            mult_load.wait()
            lzb[...] = jnp.dot(ebuf[1], mult[0], preferred_element_type=f32).astype(bf16)

        is_comp, a_now = t == t_comp[0], 0
        for a in range(1, row_blocks):
            a_now = jnp.where(t >= t_comp[a], a, a_now)
            is_comp = is_comp | (t == t_comp[a])

        @pl.when(is_comp)
        def _():
            multipliers(a_now)

        @pl.when(t == t_y)
        def _():
            w = wacc[0:1] + wacc[1:2] + wacc[2:3]
            cx[col_blocks:col_blocks + 1, :] = w[:, :size]
            cx[col_blocks + 1:col_blocks + 2, :] = w[:, size:]

        @pl.when(t == t_y + APART * (depth_z - 1 - z))
        def _():
            ct[...] = cx[...]

            @pl.when(z < depth_z - 1)
            def _():
                c_down().wait_recv()
                ct[...] += cdb[...]

            @pl.when(z > 0)
            def _():
                c_down().start()

            @pl.when(z == 0)
            def _():
                c_y().start()

        @pl.when(t == jnp.where(z == 0, t_mid, t_up + z - 1))
        def _():
            @pl.when(z == 0)
            def _():
                c_y().wait_recv()
                cub[...] = ct[...] + cyb[...]

            @pl.when(z > 0)
            def _():
                c_up().wait_recv()

            @pl.when(z < depth_z - 1)
            def _():
                c_up().start()

            for band in range(2):
                r = col_blocks + band
                wsplit[band] = split_rows([cx[r:r + 1, :], cub[r:r + 1, :]], f32, bf16)

        unit_now = (t >= t_late) & (t < t_late + n_unit - early)
        j_now = t - t_late + early
        if early:
            is_early = (t >= t_early) & (t < t_early + early)
            unit_now = unit_now | is_early
            j_now = jnp.where(is_early, t - t_early, j_now)

        @pl.when((t == t_early - 1) & (x == 0) & (z > 0) & (depth_x > 1))
        def _():
            for s in range(LENT):
                hand_on(s).wait_send()

        @pl.when(unit_now)
        def _():
            update(j_now)

    for h in range(n_group):
        unit_in(n_check + n_unit + h).wait()

    @pl.when(lent(n_sub - 1))
    def _():
        for s in range(LENT):
            t = n_sub - LENT + s

            @pl.when(z == 0)
            def _():
                lend(s).wait_send()
                u_across(t).wait_send()

            @pl.when(z > 0)
            def _():
                u_up(t).wait_recv()

    @pl.loop(SUBS * n_done, n_sub)
    def _(t):
        other_u(t)

    @pl.when(z > 0)
    def _():
        @pl.loop(SUBS * n_done, n_sub)
        def _(t):
            u_sent(t)

    @pl.when(x < depth_x - 1)
    def _():
        e_beyond().wait_send()

    e_sibling().wait_send()

    @pl.when(z == 0)
    def _():
        c_y().wait_send()

    @pl.when(z > 0)
    def _():
        c_down().wait_send()

    @pl.when(z < depth_z - 1)
    def _():
        c_up().wait_send()


def finish(dims, done, ubuf, lcat, lzb, crow, trow, wsplit, last, out, gout, tout,
           ucat, buf, outsem, donesem):
    row_blocks, col_blocks, size = dims
    f32, bf16 = jnp.float32, jnp.bfloat16
    half = size // 2
    group, n_group, n_done = parts(row_blocks, col_blocks)
    n_loads = n_group * (col_blocks + n_done)

    def unit_out(h):
        return pltpu.make_async_copy(buf.at[h], out.at[pl.ds(h * group, group), n_done], outsem.at[h])

    def done_out(m):
        return pltpu.make_async_copy(done.at[m], out.at[:, m], donesem.at[m])

    for m in range(n_done):
        done_out(m).start()

    def sums(m, upper, lower):
        own, everyone = sums_of((wsplit[0], wsplit[1]), upper, lower)
        gout[m] = crow[pl.ds(m, 1), :] - own
        tout[pl.ds(m, 1), :] = trow[pl.ds(m, 1), :] - everyone

    ucat[:size, :] = ubuf[n_done, 0]
    product = jnp.dot(lzb[...], ubuf[n_done, 0], preferred_element_type=f32)
    ucat[size:, :] = (ubuf[n_done, 1].astype(f32) - product).astype(bf16)
    for h in range(n_group):
        slot = (n_loads + h) % 2

        @pl.loop(0, group, unroll=True)
        def _(b):
            for c in range(2):
                cols = slice(c * half, (c + 1) * half)
                product = jnp.dot(lcat[h * group + b], ucat[:, cols], preferred_element_type=f32)
                buf[h, b, :, cols] = (last[slot, b, :, cols].astype(f32) - product).astype(bf16)

        unit_out(h).start()

    @pl.loop(0, n_done)
    def _(m):
        sums(m, ubuf[m, 0], ubuf[m, 1])

    sums(n_done, ucat[:size, :], ucat[size:, :])
    for m in range(n_done):
        done_out(m).wait()
    for h in range(n_group):
        unit_out(h).wait()


def local(matrix, multiplier, checksum_weight):
    row_blocks, size, col_blocks, _ = matrix.shape
    grid_rows, grid_cols = lax.axis_size("row"), lax.axis_size("col")
    bf16, f32 = jnp.bfloat16, jnp.float32
    group, n_group, n_done = parts(row_blocks, col_blocks)
    n_sub = SUBS * col_blocks
    c_rows = -(-(col_blocks + 2) // 8) * 8
    dma = pltpu.SemaphoreType.DMA
    vmem = pl.BlockSpec(memory_space=pltpu.VMEM)
    hbm = pl.BlockSpec(memory_space=pltpu.HBM)
    tiles = matrix.transpose(0, 2, 1, 3)
    sums = pltpu.VMEM((c_rows, size), f32)
    held = pl.pallas_call(
        functools.partial(gather, (grid_rows, grid_cols, row_blocks, col_blocks, size)),
        out_shape=(
            pltpu.VMEM((n_done, row_blocks, size, size), bf16),
            pltpu.VMEM((col_blocks, 2, size, size), bf16),
            pltpu.VMEM((row_blocks, size, 2 * size), bf16),
            pltpu.VMEM((size, size), bf16),
            sums,
            sums,
            pltpu.VMEM((2, 16, size), bf16),
            pltpu.VMEM((2, group, size, size), bf16),
        ),
        in_specs=[hbm, hbm, hbm],
        out_specs=(vmem,) * 8,
        scratch_shapes=[
            pltpu.VMEM(multiplier.shape, bf16),
            pltpu.VMEM(checksum_weight.shape, f32),
            pltpu.VMEM((2, size, size), bf16),
            pltpu.VMEM((row_blocks, size, 128), f32),
            pltpu.VMEM((16, 2 * size), f32),
            sums, sums, sums,
            dma((2,)), dma((2, n_sub)), dma((n_sub,)), dma((n_sub,)), dma((LENT,)), dma((LENT,)),
            dma((2, row_blocks)), dma((row_blocks,)), dma((row_blocks,)),
            dma((2,)), dma((1,)), dma((1,)),
            dma((2,)), dma((3,)), dma((3,)),
        ],
        compiler_params=pltpu.CompilerParams(
            collective_id=0, has_side_effects=True, vmem_limit_bytes=8 * 1024 * 1024),
    )(tiles, multiplier, checksum_weight)
    held = [pltpu.with_memory_space_constraint(v, pltpu.VMEM) for v in held]
    out, gout, total = pl.pallas_call(
        functools.partial(finish, (row_blocks, col_blocks, size)),
        out_shape=(
            jax.ShapeDtypeStruct(tiles.shape, bf16),
            jax.ShapeDtypeStruct((col_blocks, 1, size), f32),
            jax.ShapeDtypeStruct((col_blocks, size), f32),
        ),
        in_specs=[vmem] * 8,
        out_specs=(hbm, vmem, vmem),
        scratch_shapes=[
            pltpu.VMEM((2 * size, size), bf16),
            pltpu.VMEM((n_group, group, size, size), bf16),
            dma((n_group,)), dma((n_done,)),
        ],
        compiler_params=pltpu.CompilerParams(vmem_limit_bytes=8 * 1024 * 1024),
    )(*held)
    return (out.transpose(0, 2, 1, 3), gout.transpose(1, 0, 2), total)


def solution(mesh):
    in_specs = (P(None, "row", None, "col"), P(), P(None, "row"))
    out_specs = (P(None, "row", None, "col"), P("row", None, "col"), P(None, "col"))
    return jax.shard_map(local, mesh=mesh, in_specs=in_specs, out_specs=out_specs, check_vma=False)
```

```python
import functools

import jax
import jax.numpy as jnp
from jax import lax
from jax.experimental import pallas as pl
from jax.experimental.pallas import tpu as pltpu
from jax.sharding import PartitionSpec as P

SUBS = 4
APART = 3
AHEAD = 3
LENT = 2
MESH = pl.DeviceIdType.MESH


def parts(row_blocks, col_blocks):
    group = row_blocks // 2 if row_blocks % 2 == 0 else row_blocks
    return group, row_blocks // group, col_blocks - 1


def split_rows(rows, f32, bf16):
    n = rows[0].shape[1]
    index = lax.broadcasted_iota(jnp.int32, (16, n), 0)
    out = jnp.zeros((16, n), f32)
    for i, row in enumerate(rows):
        rest = row
        for j in range(3):
            piece = rest.astype(bf16).astype(f32)
            out = jnp.where(index == 3 * i + j, jnp.broadcast_to(piece, (16, n)), out)
            rest = rest - piece
    return out.astype(bf16)


def sums_of(weights, upper, lower):
    f32 = jnp.float32
    p = jnp.dot(weights[0], upper, preferred_element_type=f32)
    p = p + jnp.dot(weights[1], lower, preferred_element_type=f32)
    return p[0:1] + p[1:2] + p[2:3], p[3:4] + p[4:5] + p[5:6]


def gather(dims, mt, mult_in, g_in, done, ubuf, lcat, lzb, cx, cub, wsplit, min_,
           mult, g, ebuf, gcol, wacc, cyb, ct, cdb,
           gsem, usem, uzs, uys, vbs, vxs, lsem, lxs, lks, esem, exs, eks, insem, cs, cr):
    grid_rows, grid_cols, row_blocks, col_blocks, size = dims
    f32, bf16 = jnp.float32, jnp.bfloat16
    sub, half = size // SUBS, size // 2
    group, n_group, n_done = parts(row_blocks, col_blocks)
    me_r, me_c = lax.axis_index("row"), lax.axis_index("col")
    z, y, x, k = me_r // 2, me_r % 2, me_c // 2, me_c % 2
    depth_z, depth_x = grid_rows // 2, grid_cols // 2
    up, down, across = me_r + 2, me_r - 2, me_r + 1 - 2 * y
    beyond, before, sibling = me_c + 2, me_c - 2, me_c + 1 - 2 * k
    n_sub = SUBS * col_blocks
    n_check, n_unit = n_group * col_blocks, n_group * n_done
    zero = jnp.zeros((), bf16)

    first_l = row_blocks // 2
    t_item = [SUBS * (i + 1) for i in range(row_blocks + 1)]
    t_e = t_item[first_l]
    t_l = [t_item[a] if a < first_l else t_item[a + 1] for a in range(row_blocks)]
    t_comp = [t_e + 1 + a if a < first_l else t_item[a + 1] + 1 for a in range(row_blocks)]
    t_mine = SUBS + 2
    early = min(5, n_done) if n_group == 2 else 0
    t_early = t_e + 1 + first_l
    t_late = t_comp[-1] + 2
    t_y = t_comp[-1] + 1
    t_mid = t_y + APART * (depth_z - 1) + AHEAD + 1
    t_up = max(n_sub - 1, t_mid + AHEAD)
    n_step = max(n_sub, t_up + depth_z - 1, t_late + n_unit - early)

    def remote(ref, send, recv, axis, to, dst=None):
        return pltpu.make_async_remote_copy(
            src_ref=ref, dst_ref=ref if dst is None else dst, send_sem=send, recv_sem=recv,
            device_id={axis: to}, device_id_type=MESH)

    def u_ref(band, t):
        return ubuf.at[t // SUBS, band, pl.ds(pl.multiple_of((t % SUBS) * sub, sub), sub), :]

    def u_load(t):
        rows = pl.ds(pl.multiple_of((t % SUBS) * sub, sub), sub)
        return pltpu.make_async_copy(mt.at[0, t // SUBS, rows, :], u_ref(y, t), usem.at[y, t])

    def u_up(t):
        return remote(u_ref(y, t), uzs.at[t], usem.at[y, t], "row", up)

    def u_across(t):
        return remote(u_ref(y, t), uys.at[t], usem.at[y, t], "row", across)

    def u_other(t):
        return remote(u_ref(1 - y, t), uys.at[t], usem.at[1 - y, t], "row", across)

    def lent(t):
        return (x == 1) & (k == y) & (t >= n_sub - LENT)

    def carried(t):
        return (x == 0) & (k == y) & (t >= SUBS - LENT) & (t < SUBS)

    def mine(t):
        return jnp.logical_not(lent(t)) & ((x > 0) | (k != y) | (t >= SUBS - LENT))

    def lend(s):
        t = SUBS - LENT + s
        return remote(u_ref(y, n_sub - LENT + s), vbs.at[s], usem.at[y, t], "col", before, u_ref(y, t))

    def hand_on(s):
        t = n_sub - LENT + s
        return remote(u_ref(k, SUBS - LENT + s), vxs.at[s], usem.at[k, t], "col", beyond, u_ref(k, t))

    def u_sent(t):
        @pl.when(mine(t))
        def _():
            @pl.when(z < depth_z - 1)
            def _():
                u_up(t).wait_send()

            u_across(t).wait_send()

    def l_ref(band, a):
        return lcat.at[a, :, pl.ds(pl.multiple_of(band * size, size), size)]

    def l_load(a):
        return pltpu.make_async_copy(mt.at[a, 0], l_ref(k, a), lsem.at[k, a])

    def l_beyond(a):
        return remote(l_ref(k, a), lxs.at[a], lsem.at[k, a], "col", beyond)

    def l_sibling(a):
        return remote(l_ref(k, a), lks.at[a], lsem.at[k, a], "col", sibling)

    def l_other(a):
        return remote(l_ref(1 - k, a), lks.at[a], lsem.at[1 - k, a], "col", sibling)

    def relay_l(a):
        l_beyond(a).wait_recv()

        @pl.when(x < depth_x - 1)
        def _():
            l_beyond(a).start()

        l_sibling(a).start()

    def e_beyond():
        return remote(ebuf.at[1 - k], exs.at[0], esem.at[1 - k], "col", beyond)

    def e_sibling():
        return remote(ebuf.at[1 - k], eks.at[0], esem.at[1 - k], "col", sibling)

    def e_other():
        return remote(ebuf.at[k], eks.at[0], esem.at[k], "col", sibling)

    def send_e():
        @pl.when(x < depth_x - 1)
        def _():
            e_beyond().start()

        e_sibling().start()

    def c_y():
        return remote(ct, cs.at[0], cr.at[0], "row", across, cyb)

    def c_down():
        return remote(ct, cs.at[1], cr.at[1], "row", down, cdb)

    def c_up():
        return remote(cub, cs.at[2], cr.at[2], "row", up)

    def unit_of(j):
        if n_group == 1:
            return j, 0 * j
        rest = j - 2 * early
        m = jnp.where(j < early, j, jnp.where(rest < 0, j - early, early + rest // 2))
        return m, jnp.where(j < early, 0, jnp.where(rest < 0, 1, rest % 2))

    def unit_in(i):
        check = i < n_check
        m, h = unit_of(i - n_check)
        last = i - n_check - n_unit
        m = jnp.where(check, i // n_group, jnp.where(last < 0, m, n_done))
        h = jnp.where(check, i % n_group, jnp.where(last < 0, h, last))
        return pltpu.make_async_copy(mt.at[pl.ds(h * group, group), m], min_.at[i % 2], insem.at[i % 2])

    def next_in(i):
        @pl.when(i + 2 < n_check + n_unit + n_group)
        def _():
            unit_in(i + 2).start()

    barrier = pltpu.get_barrier_semaphore()
    i32 = jnp.int32
    for axis, to, there in (("row", up, z < depth_z - 1), ("row", down, z > 0), ("row", across, None),
                            ("col", beyond, x < depth_x - 1), ("col", before, x > 0), ("col", sibling, None)):
        if there is None:
            pl.semaphore_signal(barrier, inc=1, device_id={axis: to}, device_id_type=MESH)
        else:
            @pl.when(there)
            def _():
                pl.semaphore_signal(barrier, inc=1, device_id={axis: to}, device_id_type=MESH)

    @pl.when(z == 0)
    def _():
        for t in range(n_sub - LENT, n_sub):
            u_load(t).start()

        @pl.loop(0, n_sub - LENT)
        def _(t):
            @pl.when(mine(t) & jnp.logical_not(carried(t)))
            def _():
                u_load(t).start()

    @pl.when(x == 0)
    def _():
        for a in range(row_blocks):
            l_load(a).start()

    g_load = pltpu.make_async_copy(g_in, g, gsem.at[0])
    mult_load = pltpu.make_async_copy(mult_in, mult, gsem.at[1])
    g_load.start()
    mult_load.start()
    unit_in(0).start()
    unit_in(1).start()

    g_load.wait()
    for a in range(row_blocks):
        gcol[a] = jnp.broadcast_to(g[a:a + 1, :], (128, size)).T
    cx[...] = jnp.zeros_like(cx)
    wacc[...] = jnp.zeros_like(wacc)

    pl.semaphore_wait(barrier, 2 + (z < depth_z - 1).astype(i32) + (z > 0).astype(i32)
                      + (x < depth_x - 1).astype(i32) + (x > 0).astype(i32))

    def send_u(t):
        @pl.when(mine(t))
        def _():
            u_load(t).wait()
            u_up(t).start()
            u_across(t).start()

    @pl.when((z == 0) & lent(n_sub - 1))
    def _():
        for s in range(LENT):
            t = n_sub - LENT + s
            u_load(t).wait()
            lend(s).start()
            u_across(t).start()

    @pl.when(z == 0)
    def _():
        @pl.loop(0, SUBS - LENT)
        def _(t):
            send_u(t)

    @pl.when(x == 0)
    def _():
        for a in range(row_blocks):
            l_load(a).wait()
            if a < first_l:
                @pl.when(x < depth_x - 1)
                def _():
                    l_beyond(a).start()
            l_sibling(a).start()

    @pl.when(z == 0)
    def _():
        @pl.loop(SUBS - LENT, AHEAD)
        def _(t):
            send_u(t)

    def relay_u(t):
        @pl.when((z > 0) & mine(t))
        def _():
            u_up(t).wait_recv()

            @pl.when(z < depth_z - 1)
            def _():
                u_up(t).start()

            u_across(t).start()

            @pl.when(carried(t) & (depth_x > 1))
            def _():
                hand_on(t - (SUBS - LENT)).start()

        @pl.when(z == 0)
        def _():
            @pl.when(t + AHEAD < n_sub)
            def _():
                send_u(t + AHEAD)

            u_sent(t)

    def other_u(t):
        u_other(t).wait_recv()

    def check(i):
        m, h, slot = i // n_group, i % n_group, i % 2
        unit_in(i).wait()
        step = size // 8
        total = jnp.zeros((8, size), f32)
        for b in range(group):
            def body(s, acc, b=b):
                rows = pl.ds(pl.multiple_of(s * step, step), step)
                weight = gcol[h * group + b, rows, :]
                weight = jnp.concatenate([weight] * (size // 128), axis=1)
                value = min_[slot, b, rows, :].astype(f32) * weight
                return acc + jnp.sum(value.reshape(step // 8, 8, size), axis=0)
            total = lax.fori_loop(0, 8, body, total)
        next_in(i)
        cx[pl.ds(m, 1), :] += jnp.sum(total, axis=0, keepdims=True)

    def multipliers(a):
        l_other(a).wait_recv()

        @pl.when(x < depth_x - 1)
        def _():
            l_beyond(a).wait_send()

        l_sibling(a).wait_send()
        block_row = a * grid_rows + me_r
        first = jnp.dot(lcat[a, :, :size], mult[0], preferred_element_type=f32).astype(bf16)
        first = jnp.where(block_row > 0, first, zero)
        lcat[a, :, :size] = first
        product = jnp.dot(first, ebuf[0], preferred_element_type=f32)
        column = (lcat[a, :, size:].astype(f32) - product).astype(bf16)
        second = jnp.dot(column, mult[1], preferred_element_type=f32).astype(bf16)
        lcat[a, :, size:] = jnp.where(block_row > 1, second, zero)
        weights = split_rows([g[pl.ds(a, 1), :]], f32, bf16)
        wacc[...] += jnp.dot(weights, lcat[a], preferred_element_type=f32)

    def update(j):
        i = n_check + j
        m, h = unit_of(j)
        slot = i % 2
        block_col = m * grid_cols + me_c

        @pl.when(h == 0)
        def _():
            @pl.when((m > 0) | (x > 0))
            def _():
                for s in range(SUBS):
                    other_u(m * SUBS + s)

            @pl.when(z > 0)
            def _():
                for s in range(SUBS):
                    u_sent(m * SUBS + s)

            first = jnp.where(block_col > 0, ubuf[m, 0], zero)
            ubuf[m, 0] = first
            product = jnp.dot(lzb[...], first, preferred_element_type=f32)
            second = (ubuf[m, 1].astype(f32) - product).astype(bf16)
            ubuf[m, 1] = jnp.where(block_col > 1, second, zero)

        unit_in(i).wait()

        @pl.loop(0, group, unroll=True)
        def _(b):
            a = h * group + b
            for c in range(2):
                cols = slice(c * half, (c + 1) * half)
                upper = ubuf[m, :, :, cols].reshape(2 * size, half)
                product = jnp.dot(lcat[a], upper, preferred_element_type=f32)
                done[m, a, :, cols] = (min_[slot, b, :, cols].astype(f32) - product).astype(bf16)

        next_in(i)

        @pl.when(m == 0)
        def _():
            for band in range(2):
                @pl.when(me_c == band)
                def _():
                    @pl.loop(0, group)
                    def _(b):
                        a = h * group + b

                        @pl.when(a * grid_rows + me_r > band)
                        def _():
                            done[0, a] = lcat[a, :, band * size:(band + 1) * size]

    n_first = -(-n_check // 2)

    @pl.loop(0, n_step)
    def _(t):
        @pl.when(t < n_sub)
        def _():
            relay_u(t)

        @pl.when(t == t_mine)
        def _():
            @pl.when(x == 0)
            def _():
                @pl.when(k == y)
                def _():
                    for s in range(SUBS):
                        other_u(s)

                @pl.when(k != y)
                def _():
                    for s in range(LENT):
                        other_u(SUBS - LENT + s)

                        @pl.when((z > 0) & (depth_x > 1))
                        def _():
                            hand_on(s).start()

                ebuf[1 - k] = ubuf[0, 1 - k]
                send_e()

                @pl.when(x < depth_x - 1)
                def _():
                    for a in range(first_l, row_blocks):
                        l_beyond(a).start()

        @pl.when(x > 0)
        def _():
            for a in range(row_blocks):
                @pl.when(t == t_l[a])
                def _():
                    relay_l(a)

            @pl.when(t == t_e)
            def _():
                e_beyond().wait_recv()
                send_e()

        @pl.when(t < n_first)
        def _():
            check(2 * t)
            if n_check % 2 == 0:
                check(2 * t + 1)
            else:
                @pl.when(2 * t + 1 < n_check)
                def _():
                    check(2 * t + 1)

        @pl.when(t == t_e + 1)
        def _():
            e_other().wait_recv()
            mult_load.wait()
            lzb[...] = jnp.dot(ebuf[1], mult[0], preferred_element_type=f32).astype(bf16)

        is_comp, a_now = t == t_comp[0], 0
        for a in range(1, row_blocks):
            a_now = jnp.where(t >= t_comp[a], a, a_now)
            is_comp = is_comp | (t == t_comp[a])

        @pl.when(is_comp)
        def _():
            multipliers(a_now)

        @pl.when(t == t_y)
        def _():
            w = wacc[0:1] + wacc[1:2] + wacc[2:3]
            cx[col_blocks:col_blocks + 1, :] = w[:, :size]
            cx[col_blocks + 1:col_blocks + 2, :] = w[:, size:]

        @pl.when(t == t_y + APART * (depth_z - 1 - z))
        def _():
            ct[...] = cx[...]

            @pl.when(z < depth_z - 1)
            def _():
                c_down().wait_recv()
                ct[...] += cdb[...]

            @pl.when(z > 0)
            def _():
                c_down().start()

            @pl.when(z == 0)
            def _():
                c_y().start()

        @pl.when(t == jnp.where(z == 0, t_mid, t_up + z - 1))
        def _():
            @pl.when(z == 0)
            def _():
                c_y().wait_recv()
                cub[...] = ct[...] + cyb[...]

            @pl.when(z > 0)
            def _():
                c_up().wait_recv()

            @pl.when(z < depth_z - 1)
            def _():
                c_up().start()

            for band in range(2):
                r = col_blocks + band
                wsplit[band] = split_rows([cx[r:r + 1, :], cub[r:r + 1, :]], f32, bf16)

        unit_now = (t >= t_late) & (t < t_late + n_unit - early)
        j_now = t - t_late + early
        if early:
            is_early = (t >= t_early) & (t < t_early + early)
            unit_now = unit_now | is_early
            j_now = jnp.where(is_early, t - t_early, j_now)

        @pl.when((t == t_early - 1) & (x == 0) & (z > 0) & (depth_x > 1))
        def _():
            for s in range(LENT):
                hand_on(s).wait_send()

        @pl.when(unit_now)
        def _():
            update(j_now)

    for h in range(n_group):
        unit_in(n_check + n_unit + h).wait()

    @pl.when(lent(n_sub - 1))
    def _():
        for s in range(LENT):
            t = n_sub - LENT + s

            @pl.when(z == 0)
            def _():
                lend(s).wait_send()
                u_across(t).wait_send()

            @pl.when(z > 0)
            def _():
                u_up(t).wait_recv()

    @pl.loop(SUBS * n_done, n_sub)
    def _(t):
        other_u(t)

    @pl.when(z > 0)
    def _():
        @pl.loop(SUBS * n_done, n_sub)
        def _(t):
            u_sent(t)

    @pl.when(x < depth_x - 1)
    def _():
        e_beyond().wait_send()

    e_sibling().wait_send()

    @pl.when(z == 0)
    def _():
        c_y().wait_send()

    @pl.when(z > 0)
    def _():
        c_down().wait_send()

    @pl.when(z < depth_z - 1)
    def _():
        c_up().wait_send()


def finish(dims, done, ubuf, lcat, lzb, crow, trow, wsplit, last, out, gout, tout,
           ucat, buf, outsem, donesem):
    row_blocks, col_blocks, size = dims
    f32, bf16 = jnp.float32, jnp.bfloat16
    half = size // 2
    group, n_group, n_done = parts(row_blocks, col_blocks)
    n_loads = n_group * (col_blocks + n_done)

    def unit_out(h):
        return pltpu.make_async_copy(buf.at[h], out.at[pl.ds(h * group, group), n_done], outsem.at[h])

    def done_out(m, a):
        return pltpu.make_async_copy(done.at[m, a], out.at[a, m], donesem.at[m, a])

    @pl.loop(0, n_done)
    def _(m):
        for a in range(row_blocks):
            done_out(m, a).start()

    def sums(m, upper, lower):
        own, everyone = sums_of((wsplit[0], wsplit[1]), upper, lower)
        gout[m] = crow[pl.ds(m, 1), :] - own
        tout[pl.ds(m, 1), :] = trow[pl.ds(m, 1), :] - everyone

    ucat[:size, :] = ubuf[n_done, 0]
    product = jnp.dot(lzb[...], ubuf[n_done, 0], preferred_element_type=f32)
    ucat[size:, :] = (ubuf[n_done, 1].astype(f32) - product).astype(bf16)
    for h in range(n_group):
        slot = (n_loads + h) % 2

        @pl.loop(0, group, unroll=True)
        def _(b):
            for c in range(2):
                cols = slice(c * half, (c + 1) * half)
                product = jnp.dot(lcat[h * group + b], ucat[:, cols], preferred_element_type=f32)
                buf[h, b, :, cols] = (last[slot, b, :, cols].astype(f32) - product).astype(bf16)

        unit_out(h).start()

    @pl.loop(0, n_done)
    def _(m):
        sums(m, ubuf[m, 0], ubuf[m, 1])

    sums(n_done, ucat[:size, :], ucat[size:, :])
    @pl.loop(0, n_done)
    def _(m):
        for a in range(row_blocks):
            done_out(m, a).wait()

    for h in range(n_group):
        unit_out(h).wait()


def local(matrix, multiplier, checksum_weight):
    row_blocks, size, col_blocks, _ = matrix.shape
    grid_rows, grid_cols = lax.axis_size("row"), lax.axis_size("col")
    bf16, f32 = jnp.bfloat16, jnp.float32
    group, n_group, n_done = parts(row_blocks, col_blocks)
    n_sub = SUBS * col_blocks
    c_rows = -(-(col_blocks + 2) // 8) * 8
    dma = pltpu.SemaphoreType.DMA
    vmem = pl.BlockSpec(memory_space=pltpu.VMEM)
    hbm = pl.BlockSpec(memory_space=pltpu.HBM)
    tiles = matrix.transpose(0, 2, 1, 3)
    sums = pltpu.VMEM((c_rows, size), f32)
    held = pl.pallas_call(
        functools.partial(gather, (grid_rows, grid_cols, row_blocks, col_blocks, size)),
        out_shape=(
            pltpu.VMEM((n_done, row_blocks, size, size), bf16),
            pltpu.VMEM((col_blocks, 2, size, size), bf16),
            pltpu.VMEM((row_blocks, size, 2 * size), bf16),
            pltpu.VMEM((size, size), bf16),
            sums,
            sums,
            pltpu.VMEM((2, 16, size), bf16),
            pltpu.VMEM((2, group, size, size), bf16),
        ),
        in_specs=[hbm, hbm, hbm],
        out_specs=(vmem,) * 8,
        scratch_shapes=[
            pltpu.VMEM(multiplier.shape, bf16),
            pltpu.VMEM(checksum_weight.shape, f32),
            pltpu.VMEM((2, size, size), bf16),
            pltpu.VMEM((row_blocks, size, 128), f32),
            pltpu.VMEM((16, 2 * size), f32),
            sums, sums, sums,
            dma((2,)), dma((2, n_sub)), dma((n_sub,)), dma((n_sub,)), dma((LENT,)), dma((LENT,)),
            dma((2, row_blocks)), dma((row_blocks,)), dma((row_blocks,)),
            dma((2,)), dma((1,)), dma((1,)),
            dma((2,)), dma((3,)), dma((3,)),
        ],
        compiler_params=pltpu.CompilerParams(
            collective_id=0, has_side_effects=True, vmem_limit_bytes=8 * 1024 * 1024),
    )(tiles, multiplier, checksum_weight)
    held = [pltpu.with_memory_space_constraint(v, pltpu.VMEM) for v in held]
    out, gout, total = pl.pallas_call(
        functools.partial(finish, (row_blocks, col_blocks, size)),
        out_shape=(
            jax.ShapeDtypeStruct(tiles.shape, bf16),
            jax.ShapeDtypeStruct((col_blocks, 1, size), f32),
            jax.ShapeDtypeStruct((col_blocks, size), f32),
        ),
        in_specs=[vmem] * 8,
        out_specs=(hbm, vmem, vmem),
        scratch_shapes=[
            pltpu.VMEM((2 * size, size), bf16),
            pltpu.VMEM((n_group, group, size, size), bf16),
            dma((n_group,)), dma((n_done, row_blocks)),
        ],
        compiler_params=pltpu.CompilerParams(vmem_limit_bytes=8 * 1024 * 1024),
    )(*held)
    return (out.transpose(0, 2, 1, 3), gout.transpose(1, 0, 2), total)


def solution(mesh):
    in_specs = (P(None, "row", None, "col"), P(), P(None, "row"))
    out_specs = (P(None, "row", None, "col"), P("row", None, "col"), P(None, "col"))
    return jax.shard_map(local, mesh=mesh, in_specs=in_specs, out_specs=out_specs, check_vma=False)
```
